32 devices in a mesh: groups: 2 (over y), tok: 16 (over z, x, core).
Axes of the slice: x: 2, y: 2, z: 4, core: 2. Of those that a mesh axis runs over, the one named last changes fastest.
Arguments:
- hidden_rows: bfloat16 [4096, 3584], P(('groups', 'tok')), parts along dimension 0, may hold values from -6 to 6
- queries: bfloat16 [4096, 1792], P(('groups', 'tok')), parts along dimension 0, may hold values from -400 to 400
- labels: int32 [4096], P(('groups', 'tok')), parts along dimension 0, may hold values from 0 to 1, as said below
- doc_lengths: int32 [32], P('groups'), parts along dimension 0, may hold values from 1 to 1152, as said below
- kv_weights: bfloat16 [2, 3584, 512], replicated, may hold values from -0.09375 to 0.09375
- key_gains: float32 [2, 128], replicated, may hold values from 0.1 to 1.9
Outputs:
- attended: bfloat16 [4096, 1792], P(('groups', 'tok')), parts along dimension 0
The draws below stay inside these ranges and needn't reach their ends.
There are 2 independent parts, one for each index of `groups`. The reference program is written for one: setup_inputs(seed, part) draws one part's arguments, and reference() takes and returns one part's arrays. A program takes and returns all parts, laid end to end along the dimension named above; an argument that names none is the same for every part. Nothing has to cross between parts.
Inputs may be any that keep to these rules, and one draw needn't show every extreme that they name: `labels`: 0 marks an understanding token, 1 a generation token; generation tokens come in runs. `doc_lengths`: the lengths sum to 2048; the last sample is the longest, with 1152 tokens.
All inputs are finite; a program needn't handle non-finite values.
Results may differ from the reference program's by a relative error of at most 0.0055.
The reference program's roundings to bfloat16 on the way (of `weight16`) count: a program that leaves them out, or rounds other values in their place, can miss the bound.
Values may be sent and summed in bfloat16 or wider, within the bound.
A program may use at most 128 MiB of HBM per device.

```python
import math
import jax
import jax.numpy as jnp
from jax import lax

D = 3584
HEADS = 14
KVH = 2
HD = 128
DOCS = 16
TOK_DEV = 128
TOKENS = 2048
MOST_LEN = 1152


def draw_queries(key, part):
    normal_part = jax.random.normal(jax.random.fold_in(key, 11), (TOKENS, HEADS * HD), jnp.float32)
    values = jnp.clip(normal_part, -6.0, 6.0)
    return values.astype(jnp.bfloat16)


def draw_labels(key, part):
    toggles = jax.random.randint(jax.random.fold_in(key, 21), (TOKENS,), 0, 4 * TOK_DEV)
    flips = jnp.where(toggles == 0, 1, 0).astype(jnp.int32)
    base = (jnp.cumsum(flips) % 2).astype(jnp.int32)
    positions = jnp.arange(TOKENS, dtype=jnp.int32)
    device_of = positions // TOK_DEV
    within = positions % TOK_DEV
    device_total = TOKENS // TOK_DEV
    middle = device_total // 2
    forced_one = (device_of == middle - 1) | (device_of == device_total - 2)
    forced_zero = ((device_of == middle) | (device_of == device_total - 1)) & (within == 0)
    labels = jnp.where(forced_one, 1, base)
    labels = jnp.where(forced_zero, 0, labels)
    return labels.astype(jnp.int32)


def draw_doc_lengths(key, part):
    short_total = TOKENS - MOST_LEN
    picks = jax.random.permutation(jax.random.fold_in(key, 31), short_total - 1)[:DOCS - 2] + 1
    cuts = jnp.sort(picks.astype(jnp.int32))
    bounds = jnp.concatenate([jnp.zeros((1,), jnp.int32), cuts, jnp.full((1,), short_total, jnp.int32)])
    shorter = (bounds[1:] - bounds[:-1]).astype(jnp.int32)
    return jnp.concatenate([shorter, jnp.full((1,), MOST_LEN, jnp.int32)]).astype(jnp.int32)


def steps_of(key, shape, shards, smallest, top_value):
    def one(axis_at, shards_of):
        heights = jax.random.uniform(jax.random.fold_in(jax.random.fold_in(key, 6), axis_at), (shards_of,), jnp.float32, smallest / len(shards), top_value / len(shards))
        return jnp.repeat(jnp.exp(heights), shape[axis_at] // shards_of).reshape((-1,) + (1,) * (len(shape) - axis_at - 1))

    loudness = one(*shards[0])
    for cut in shards[1:]:
        loudness = loudness * one(*cut)
    return loudness


def centred(stream_key, shape, width, bound, cuts=(), kind=jnp.bfloat16):
    values = width * jax.random.normal(stream_key, shape, jnp.float32)
    if cuts:
        values = values * steps_of(stream_key, shape, cuts, -0.22, 0.18)
    return jnp.clip(values, -bound, bound).astype(kind)


def setup_inputs(seed: int = 0, part: int = 0) -> dict:
    key_list = jax.random.split(jax.random.key(seed), 7)
    part_splits = jax.random.split(jax.random.fold_in(key_list[6], part), 7)
    return {
        "hidden_rows": centred(part_splits[0], (TOKENS, D), 1.0, 6.0, ((0, 16),)),
        "queries": draw_queries(jax.random.fold_in(jax.random.fold_in(key_list[6], part), 71), part),
        "labels": draw_labels(jax.random.fold_in(jax.random.fold_in(key_list[6], part), 71), part),
        "doc_lengths": draw_doc_lengths(jax.random.fold_in(jax.random.fold_in(key_list[6], part), 71), part),
        "kv_weights": centred(key_list[4], (2, D, 2 * KVH * HD), D ** -0.5, 0.09375),
        "key_gains": jnp.clip(1.0 + 0.18 * jax.random.normal(key_list[5], (2, HD), jnp.float32), 0.1, 1.9),
    }


def reference(hidden_rows, queries, labels, doc_lengths, kv_weights, key_gains):
    total_len = hidden_rows.shape[0]
    half = KVH * HD
    groups_per = HEADS // KVH
    tower_zero = jnp.dot(hidden_rows, kv_weights[0], preferred_element_type=jnp.float32)
    tower_one = jnp.dot(hidden_rows, kv_weights[1], preferred_element_type=jnp.float32)
    chosen = labels[:, None] == 1
    projected = jnp.where(chosen, tower_one, tower_zero)
    keys = projected[:, :half].reshape(total_len, KVH, HD)
    square_mean = lax.optimization_barrier(jnp.mean(keys * keys, axis=-1, keepdims=True))
    gains = jnp.where(chosen, key_gains[1][None, :], key_gains[0][None, :])
    keys = (keys * lax.rsqrt(square_mean + 1e-06) * gains[:, None, :]).astype(jnp.bfloat16)
    values = projected[:, half:].astype(jnp.bfloat16)
    positions = jnp.arange(total_len, dtype=jnp.int32)
    ends = jnp.cumsum(doc_lengths).astype(jnp.int32)
    first_pos = lax.optimization_barrier(jnp.max(jnp.where(ends[None, :] <= positions[:, None], ends[None, :], 0), axis=1))
    last_pos = lax.optimization_barrier(jnp.min(jnp.where(ends[None, :] > positions[:, None], ends[None, :], total_len), axis=1)) - 1
    zero_next = lax.cummin(jnp.where(labels == 0, positions, total_len), axis=0, reverse=True)
    reach = jnp.where(labels == 1, jnp.minimum(last_pos, zero_next - 1), positions)
    all_keys = keys.astype(jnp.float32)
    all_values = values.reshape(total_len, KVH, HD).astype(jnp.float32)
    block = math.gcd(total_len, 256)
    scale = 1.0 / HD ** 0.5

    def one_block(block_index):
        start = (block_index * block).astype(jnp.int32)
        query_rows = lax.dynamic_slice_in_dim(queries, start, block, 0).astype(jnp.float32)
        query_rows = query_rows.reshape(block, KVH, groups_per, HD)
        low = lax.dynamic_slice_in_dim(first_pos, start, block, 0)
        high = lax.dynamic_slice_in_dim(reach, start, block, 0)
        visible = (positions[None, :] >= low[:, None]) & (positions[None, :] <= high[:, None])
        visible = visible[:, None, None, :]
        scores = jnp.einsum('tkgd,skd->tkgs', query_rows, all_keys) * scale
        scores = jnp.where(visible, scores, -1e+30)
        peak = lax.optimization_barrier(jnp.max(scores, axis=-1, keepdims=True))
        weight = jnp.where(visible, jnp.exp(scores - peak), 0.0)
        summed = lax.optimization_barrier(jnp.sum(weight, axis=-1))
        weight16 = weight.astype(jnp.bfloat16).astype(jnp.float32)
        mixed = jnp.einsum('tkgs,skd->tkgd', weight16, all_values)
        result = mixed / summed[..., None]
        return result.reshape(block, HEADS * HD).astype(jnp.bfloat16)
    blocks = lax.map(one_block, jnp.arange(total_len // block, dtype=jnp.int32))
    return blocks.reshape(total_len, HEADS * HD)
```

```python
import functools
import math

import jax
import jax.numpy as jnp
from jax import lax
from jax.experimental import pallas as pl
from jax.experimental.pallas import tpu as pltpu
from jax.sharding import PartitionSpec as P

HEADS = 14
KVH = 2
HD = 128
GROUPS_PER = HEADS // KVH
HALF = KVH * HD
MESH = pl.DeviceIdType.MESH
NEG = -1e30


def kernel(
    n,
    chunk,
    labels_ref,
    lengths_ref,
    gains_ref,
    hidden_hbm,
    queries_hbm,
    weights_hbm,
    out_ref,
    hidden,
    query,
    weights,
    held,
    zeros_at,
    peak,
    summed,
    accum,
    in_sem,
    query_sem,
    weight_sem,
    send_sem,
    recv_sem,
    pass_sem,
    zsend_sem,
    zrecv_sem,
):
    rows, depth = hidden.shape
    total_len = n * rows
    me = lax.axis_index("tok")
    core = lax.rem(me, 2)
    partner = me + 1 - 2 * core
    split = n // 2 - 1
    upper = me >= split
    low = jnp.where(upper, split, 0)
    high = jnp.where(upper, n, split)
    paired = (partner >= low) & (partner < high)
    lone = jnp.where(upper, split, split - 1)
    unused = jnp.where(upper, split - 1, split)

    def block(j):
        return pl.ds(pl.multiple_of(j * rows, rows), rows)

    hidden_copy = pltpu.make_async_copy(hidden_hbm, hidden, in_sem)
    hidden_copy.start()
    chunks = depth // chunk
    weight_copies = []
    for i in range(chunks):
        part = pl.ds(i * chunk, chunk)
        copy = pltpu.make_async_copy(
            weights_hbm.at[:, part, :], weights.at[:, part, :], weight_sem.at[i]
        )
        copy.start()
        weight_copies.append(copy)
    query_copies = []
    for h in range(HEADS):
        copy = pltpu.make_async_copy(
            queries_hbm.at[:, pl.ds(h * HD, HD)],
            query.at[pl.ds(h * rows, rows), :],
            query_sem.at[h],
        )
        copy.start()
        query_copies.append(copy)

    offset = me * rows
    lane_pos = offset + lax.broadcasted_iota(jnp.int32, (1, rows), 1)
    labels = labels_ref[...]
    first_lane = jnp.zeros((1, rows), jnp.int32)
    last_lane = jnp.full((1, rows), total_len, jnp.int32)
    end = jnp.int32(0)
    for i in range(lengths_ref.shape[0]):
        end = end + lengths_ref[i]
        first_lane = jnp.maximum(first_lane, jnp.where(end <= lane_pos, end, 0))
        last_lane = jnp.minimum(last_lane, jnp.where(end > lane_pos, end, total_len))
    last_lane = last_lane - 1
    row_at = lax.broadcasted_iota(jnp.int32, (rows, rows), 0)
    lane_at = lax.broadcasted_iota(jnp.int32, (rows, rows), 1)
    diagonal = row_at == lane_at

    def to_rows(lane_values):
        spread = jnp.where(diagonal, jnp.broadcast_to(lane_values, (rows, rows)), 0)
        return jnp.sum(spread, axis=1, keepdims=True)

    first = to_rows(first_lane)
    last = to_rows(last_lane)
    label = to_rows(labels)
    zero_lane = jnp.where(labels == 0, lane_pos, total_len)
    local_zero = jnp.min(
        jnp.where(lane_at >= row_at, jnp.broadcast_to(zero_lane, (rows, rows)), total_len),
        axis=1,
        keepdims=True,
    )
    earliest = jnp.min(zero_lane, axis=1, keepdims=True)
    zeros_at[...] = jnp.full(zeros_at.shape, total_len, jnp.int32)
    zeros_at[me] = jnp.broadcast_to(earliest, (8, rows))
    held[block(unused), :] = jnp.zeros((rows, 2 * HALF), jnp.bfloat16)
    peak[...] = jnp.full(peak.shape, NEG, jnp.float32)
    summed[...] = jnp.zeros(summed.shape, jnp.float32)
    accum[...] = jnp.zeros(accum.shape, jnp.float32)

    barrier = pltpu.get_barrier_semaphore()

    @pl.loop(low, high)
    def _(d):
        @pl.when(d != me)
        def _():
            pl.semaphore_signal(barrier, inc=1, device_id={"tok": d}, device_id_type=MESH)

    def zero_copy(source, target):
        return pltpu.make_async_remote_copy(
            src_ref=zeros_at.at[source],
            dst_ref=zeros_at.at[source],
            send_sem=zsend_sem.at[target],
            recv_sem=zrecv_sem.at[source],
            device_id={"tok": target},
            device_id_type=MESH,
        )

    def own_copy(source, target):
        return pltpu.make_async_remote_copy(
            src_ref=held.at[block(source), :],
            dst_ref=held.at[block(source), :],
            send_sem=send_sem.at[target],
            recv_sem=recv_sem.at[source],
            device_id={"tok": target},
            device_id_type=MESH,
        )

    def pass_copy(source):
        return pltpu.make_async_remote_copy(
            src_ref=held.at[block(source), :],
            dst_ref=held.at[block(source), :],
            send_sem=pass_sem.at[source],
            recv_sem=recv_sem.at[source],
            device_id={"tok": partner},
            device_id_type=MESH,
        )

    hidden_copy.wait()
    projected = [jnp.zeros((rows, 2 * HALF), jnp.float32) for _ in range(2)]
    for i in range(chunks):
        weight_copies[i].wait()
        part = pl.ds(i * chunk, chunk)
        for tower in range(2):
            projected[tower] = projected[tower] + jnp.dot(
                hidden[:, part], weights[tower, part, :], preferred_element_type=jnp.float32
            )
        if i == chunks // 2:
            pl.semaphore_wait(barrier, high - low - 1)

            @pl.loop(low, me)
            def _(d):
                zero_copy(me, d).start()

    chosen = label == 1
    gains = jnp.where(chosen, gains_ref[1:2, :], gains_ref[0:1, :])
    mine = jnp.where(chosen, projected[1], projected[0])
    for g in range(KVH):
        key = mine[:, g * HD : (g + 1) * HD]
        square_mean = jnp.mean(key * key, axis=-1, keepdims=True)
        key = key * lax.rsqrt(square_mean + 1e-06) * gains
        held[block(me), g * HD : (g + 1) * HD] = key.astype(jnp.bfloat16)
    held[block(me), HALF:] = mine[:, HALF:].astype(jnp.bfloat16)

    def own_target(d):
        same = lax.rem(d, 2) == core
        return (d != me) & (same | (d == partner) | (d == lone))

    count = high - low

    @pl.loop(1, count)
    def _(k):
        d = low + lax.rem(me - low - k + count, count)

        @pl.when(own_target(d))
        def _():
            own_copy(me, d).start()

    @pl.loop(me + 1, high)
    def _(d):
        zero_copy(d, me).wait_recv()

    device_at = lax.broadcasted_iota(jnp.int32, zeros_at.shape, 0)
    later = jnp.min(jnp.where(device_at > me, zeros_at[...], total_len), axis=0)
    later = later[0:1, 0:1]
    zero_next = jnp.minimum(local_zero, later)
    row_pos = offset + lax.broadcasted_iota(jnp.int32, (rows, 1), 0)
    reach = jnp.where(label == 1, jnp.minimum(last, zero_next - 1), row_pos)
    for copy in query_copies:
        copy.wait()

    factor_of = (1.0 / HD**0.5) * math.log2(math.e)
    chip_low = low // 2
    chip_count = (high + 1) // 2 - chip_low
    my_chip = me // 2
    pair = 2 * rows

    @pl.loop(0, chip_count)
    def _(t):
        chip = chip_low + lax.rem(my_chip - chip_low + t, chip_count)
        same = 2 * chip + core
        other = 2 * chip + 1 - core

        @pl.when((same != me) & (same >= low) & (same < high))
        def _():
            own_copy(same, me).wait_recv()

            @pl.when(paired)
            def _():
                pass_copy(same).start()

        @pl.when((other >= low) & (other < high))
        def _():
            own_copy(other, me).wait_recv()

        start = pl.multiple_of(chip * pair, pair)
        key_pos = start + lax.broadcasted_iota(jnp.int32, (rows, pair), 1)
        bias = jnp.where((key_pos >= first) & (key_pos <= reach), 0.0, NEG)
        for g in range(KVH):
            group = pl.ds(g * GROUPS_PER * rows, GROUPS_PER * rows)
            keys = held[pl.ds(start, pair), g * HD : (g + 1) * HD]
            values = held[pl.ds(start, pair), HALF + g * HD : HALF + (g + 1) * HD]
            scores = lax.dot_general(
                query[group, :],
                keys,
                (((1,), (1,)), ((), ())),
                preferred_element_type=jnp.float32,
            )
            scores = scores.reshape(GROUPS_PER, rows, pair)
            scores = jnp.where(bias[None] == 0.0, scores, NEG)
            scores = scores.reshape(GROUPS_PER * rows, pair)
            old_peak = peak[group, :]
            new_peak = jnp.maximum(old_peak, jnp.max(scores, axis=-1, keepdims=True))
            weight = jnp.exp2((scores - new_peak) * factor_of)
            factor = jnp.exp2((old_peak - new_peak) * factor_of)
            peak[group, :] = new_peak
            summed[group, :] = summed[group, :] * factor + jnp.sum(weight, axis=-1, keepdims=True)
            mixed = jnp.dot(
                weight.astype(jnp.bfloat16), values, preferred_element_type=jnp.float32
            )
            accum[group, :] = accum[group, :] * factor + mixed

    for h in range(HEADS):
        head = pl.ds(h * rows, rows)
        result = accum[head, :] / summed[head, :]
        out_ref[:, h * HD : (h + 1) * HD] = result.astype(out_ref.dtype)

    @pl.loop(low, me)
    def _(d):
        zero_copy(me, d).wait_send()

    @pl.loop(low, high)
    def _(d):
        @pl.when(own_target(d))
        def _():
            own_copy(me, d).wait_send()

        @pl.when(paired & (d != me) & (lax.rem(d, 2) == core))
        def _():
            pass_copy(d).wait_send()


def solution(mesh):
    n = mesh.shape["tok"]

    def shards(hidden_rows, queries, labels, doc_lengths, kv_weights, key_gains):
        rows, depth = hidden_rows.shape
        chunk = math.gcd(depth, 512)
        any_space = pl.BlockSpec(memory_space=pl.ANY)
        vmem = pl.BlockSpec(memory_space=pltpu.VMEM)
        return pl.pallas_call(
            functools.partial(kernel, n, chunk),
            out_shape=jax.ShapeDtypeStruct(queries.shape, jnp.bfloat16),
            in_specs=[
                vmem,
                pl.BlockSpec(memory_space=pltpu.SMEM),
                vmem,
                any_space,
                any_space,
                any_space,
            ],
            out_specs=vmem,
            scratch_shapes=[
                pltpu.VMEM((rows, depth), jnp.bfloat16),
                pltpu.VMEM((HEADS * rows, HD), jnp.bfloat16),
                pltpu.VMEM(kv_weights.shape, jnp.bfloat16),
                pltpu.VMEM((n * rows, 2 * HALF), jnp.bfloat16),
                pltpu.VMEM((n, 8, rows), jnp.int32),
                pltpu.VMEM((HEADS * rows, 1), jnp.float32),
                pltpu.VMEM((HEADS * rows, 1), jnp.float32),
                pltpu.VMEM((HEADS * rows, HD), jnp.float32),
                pltpu.SemaphoreType.DMA,
                pltpu.SemaphoreType.DMA((HEADS,)),
                pltpu.SemaphoreType.DMA((depth // chunk,)),
                pltpu.SemaphoreType.DMA((n,)),
                pltpu.SemaphoreType.DMA((n,)),
                pltpu.SemaphoreType.DMA((n,)),
                pltpu.SemaphoreType.DMA((n,)),
                pltpu.SemaphoreType.DMA((n,)),
            ],
            compiler_params=pltpu.CompilerParams(collective_id=0, has_side_effects=True),
        )(labels.reshape(1, rows), doc_lengths, key_gains, hidden_rows, queries, kv_weights)

    in_specs = (
        P(("groups", "tok"), None),
        P(("groups", "tok"), None),
        P(("groups", "tok")),
        P("groups"),
        P(),
        P(),
    )
    out_specs = P(("groups", "tok"), None)
    return jax.shard_map(shards, mesh=mesh, in_specs=in_specs, out_specs=out_specs, check_vma=False)
```

```python
import functools
import math

import jax
import jax.numpy as jnp
from jax import lax
from jax.experimental import pallas as pl
from jax.experimental.pallas import tpu as pltpu
from jax.sharding import PartitionSpec as P

HEADS = 14
KVH = 2
HD = 128
GROUPS_PER = HEADS // KVH
HALF = KVH * HD
MESH = pl.DeviceIdType.MESH
NEG = -1e30


def kernel(
    n,
    chunk,
    labels_ref,
    lengths_ref,
    gains_ref,
    hidden_hbm,
    queries_hbm,
    weights_hbm,
    out_ref,
    hidden,
    query,
    weights,
    held,
    zeros_at,
    peak,
    summed,
    accum,
    in_sem,
    query_sem,
    weight_sem,
    send_sem,
    recv_sem,
    pass_sem,
    zsend_sem,
    zrecv_sem,
):
    rows, depth = hidden.shape
    total_len = n * rows
    me = lax.axis_index("tok")
    core = lax.rem(me, 2)
    partner = me + 1 - 2 * core
    split = n // 2 - 1
    upper = me >= split
    low = jnp.where(upper, split, 0)
    high = jnp.where(upper, n, split)
    paired = (partner >= low) & (partner < high)
    lone = jnp.where(upper, split, split - 1)
    unused = jnp.where(upper, split - 1, split)

    size = HALF // HD * rows + HALF

    def block(j):
        return pl.ds(pl.multiple_of(j * size, size), size)

    def part_of(j, at, length):
        return pl.ds(pl.multiple_of(j * size + at, 16), length)

    hidden_copy = pltpu.make_async_copy(hidden_hbm, hidden, in_sem)
    hidden_copy.start()
    chunks = depth // chunk
    weight_copies = []
    for i in range(chunks):
        part = pl.ds(i * chunk, chunk)
        copy = pltpu.make_async_copy(
            weights_hbm.at[:, part, :], weights.at[:, part, :], weight_sem.at[i]
        )
        copy.start()
        weight_copies.append(copy)
    query_copies = []
    for h in range(HEADS):
        copy = pltpu.make_async_copy(
            queries_hbm.at[:, pl.ds(h * HD, HD)],
            query.at[pl.ds(h * rows, rows), :],
            query_sem.at[h],
        )
        copy.start()
        query_copies.append(copy)

    offset = me * rows
    lane_pos = offset + lax.broadcasted_iota(jnp.int32, (1, rows), 1)
    labels = labels_ref[...]
    first_lane = jnp.zeros((1, rows), jnp.int32)
    last_lane = jnp.full((1, rows), total_len, jnp.int32)
    end = jnp.int32(0)
    for i in range(lengths_ref.shape[0]):
        end = end + lengths_ref[i]
        first_lane = jnp.maximum(first_lane, jnp.where(end <= lane_pos, end, 0))
        last_lane = jnp.minimum(last_lane, jnp.where(end > lane_pos, end, total_len))
    last_lane = last_lane - 1
    row_at = lax.broadcasted_iota(jnp.int32, (rows, rows), 0)
    lane_at = lax.broadcasted_iota(jnp.int32, (rows, rows), 1)
    diagonal = row_at == lane_at

    zero_lane = jnp.where(labels == 0, lane_pos, total_len)
    def to_rows(lane_values):
        spread = jnp.where(diagonal, jnp.broadcast_to(lane_values, (rows, rows)), 0)
        return jnp.sum(spread, axis=1, keepdims=True)

    label = to_rows(labels)
    local_zero = jnp.min(
        jnp.where(row_at >= lane_at, to_rows(zero_lane), total_len), axis=0, keepdims=True
    )
    earliest = jnp.min(zero_lane, axis=1, keepdims=True)
    zeros_at[...] = jnp.full(zeros_at.shape, total_len, jnp.int32)
    zeros_at[me] = jnp.broadcast_to(earliest, (8, rows))
    held[block(unused), :] = jnp.zeros((size, HD), jnp.bfloat16)
    peak[...] = jnp.full(peak.shape, NEG, jnp.float32)
    summed[...] = jnp.zeros(summed.shape, jnp.float32)
    accum[...] = jnp.zeros(accum.shape, jnp.float32)

    barrier = pltpu.get_barrier_semaphore()

    @pl.loop(low, high)
    def _(d):
        @pl.when(d != me)
        def _():
            pl.semaphore_signal(barrier, inc=1, device_id={"tok": d}, device_id_type=MESH)

    def zero_copy(source, target):
        return pltpu.make_async_remote_copy(
            src_ref=zeros_at.at[source],
            dst_ref=zeros_at.at[source],
            send_sem=zsend_sem.at[target],
            recv_sem=zrecv_sem.at[source],
            device_id={"tok": target},
            device_id_type=MESH,
        )

    def own_copy(source, target):
        return pltpu.make_async_remote_copy(
            src_ref=held.at[block(source), :],
            dst_ref=held.at[block(source), :],
            send_sem=send_sem.at[target],
            recv_sem=recv_sem.at[source],
            device_id={"tok": target},
            device_id_type=MESH,
        )

    def pass_copy(source):
        return pltpu.make_async_remote_copy(
            src_ref=held.at[block(source), :],
            dst_ref=held.at[block(source), :],
            send_sem=pass_sem.at[source],
            recv_sem=recv_sem.at[source],
            device_id={"tok": partner},
            device_id_type=MESH,
        )

    hidden_copy.wait()
    projected = [jnp.zeros((rows, 2 * HALF), jnp.float32) for _ in range(2)]
    for i in range(chunks):
        weight_copies[i].wait()
        part = pl.ds(i * chunk, chunk)
        for tower in range(2):
            projected[tower] = projected[tower] + jnp.dot(
                hidden[:, part], weights[tower, part, :], preferred_element_type=jnp.float32
            )
        if i == chunks // 2:
            pl.semaphore_wait(barrier, high - low - 1)

            @pl.loop(low, me)
            def _(d):
                zero_copy(me, d).start()

    chosen = label == 1
    gains = jnp.where(chosen, gains_ref[1:2, :], gains_ref[0:1, :])
    mine = jnp.where(chosen, projected[1], projected[0])
    for g in range(KVH):
        key = mine[:, g * HD : (g + 1) * HD]
        square_mean = jnp.mean(key * key, axis=-1, keepdims=True)
        key = key * lax.rsqrt(square_mean + 1e-06) * gains
        held[part_of(me, g * rows, rows), :] = key.astype(jnp.bfloat16)
        value = mine[:, HALF + g * HD : HALF + (g + 1) * HD]
        held[part_of(me, KVH * rows + g * HD, HD), :] = value.T.astype(jnp.bfloat16)

    def own_target(d):
        same = lax.rem(d, 2) == core
        return (d != me) & (same | (d == partner) | (d == lone))

    count = high - low

    @pl.loop(1, count)
    def _(k):
        d = low + lax.rem(me - low - k + count, count)

        @pl.when(own_target(d))
        def _():
            own_copy(me, d).start()

    @pl.loop(me + 1, high)
    def _(d):
        zero_copy(d, me).wait_recv()

    device_at = lax.broadcasted_iota(jnp.int32, zeros_at.shape, 0)
    later = jnp.min(jnp.where(device_at > me, zeros_at[...], total_len), axis=0)
    later = later[0:1, 0:1]
    zero_next = jnp.minimum(local_zero, later)
    reach = jnp.where(labels == 1, jnp.minimum(last_lane, zero_next - 1), lane_pos)
    for copy in query_copies:
        copy.wait()

    factor_of = (1.0 / HD**0.5) * math.log2(math.e)
    chip_low = low // 2
    chip_count = (high + 1) // 2 - chip_low
    my_chip = me // 2
    pair = 2 * rows

    @pl.loop(0, chip_count)
    def _(t):
        chip = chip_low + lax.rem(my_chip - chip_low + t, chip_count)
        same = 2 * chip + core
        other = 2 * chip + 1 - core

        @pl.when((same != me) & (same >= low) & (same < high))
        def _():
            own_copy(same, me).wait_recv()

            @pl.when(paired)
            def _():
                pass_copy(same).start()

        @pl.when((other >= low) & (other < high))
        def _():
            own_copy(other, me).wait_recv()

        key_pos = chip * pair + lax.broadcasted_iota(jnp.int32, (pair, rows), 0)
        visible = (key_pos >= first_lane) & (key_pos <= reach)
        bias = jnp.where(visible, 0.0, NEG)
        for g in range(KVH):
            keys = jnp.concatenate(
                [held[part_of(2 * chip + i, g * rows, rows), :] for i in range(2)], axis=0
            )
            values = jnp.concatenate(
                [held[part_of(2 * chip + i, KVH * rows + g * HD, HD), :] for i in range(2)], axis=1
            )
            for h in range(g * GROUPS_PER, (g + 1) * GROUPS_PER):
                scores = lax.dot_general(
                    keys,
                    query[h * rows : (h + 1) * rows, :],
                    (((1,), (1,)), ((), ())),
                    preferred_element_type=jnp.float32,
                )
                scores = scores + bias
                old_peak = peak[h : h + 1, :]
                new_peak = jnp.maximum(old_peak, jnp.max(scores, axis=0, keepdims=True))
                weight = jnp.exp2((scores - new_peak) * factor_of)
                factor = jnp.exp2((old_peak - new_peak) * factor_of)
                peak[h : h + 1, :] = new_peak
                summed[h : h + 1, :] = summed[h : h + 1, :] * factor + jnp.sum(
                    weight, axis=0, keepdims=True
                )
                mixed = jnp.dot(
                    values, weight.astype(jnp.bfloat16), preferred_element_type=jnp.float32
                )
                accum[h] = accum[h] * factor + mixed

    for h in range(HEADS):
        result = accum[h] * (1.0 / summed[h : h + 1, :])
        out_ref[:, h * HD : (h + 1) * HD] = result.T.astype(out_ref.dtype)

    @pl.loop(low, me)
    def _(d):
        zero_copy(me, d).wait_send()

    @pl.loop(low, high)
    def _(d):
        @pl.when(own_target(d))
        def _():
            own_copy(me, d).wait_send()

        @pl.when(paired & (d != me) & (lax.rem(d, 2) == core))
        def _():
            pass_copy(d).wait_send()


def solution(mesh):
    n = mesh.shape["tok"]

    def shards(hidden_rows, queries, labels, doc_lengths, kv_weights, key_gains):
        rows, depth = hidden_rows.shape
        assert rows == HD
        chunk = math.gcd(depth, 512)
        any_space = pl.BlockSpec(memory_space=pl.ANY)
        vmem = pl.BlockSpec(memory_space=pltpu.VMEM)
        return pl.pallas_call(
            functools.partial(kernel, n, chunk),
            out_shape=jax.ShapeDtypeStruct(queries.shape, jnp.bfloat16),
            in_specs=[
                vmem,
                pl.BlockSpec(memory_space=pltpu.SMEM),
                vmem,
                any_space,
                any_space,
                any_space,
            ],
            out_specs=vmem,
            scratch_shapes=[
                pltpu.VMEM((rows, depth), jnp.bfloat16),
                pltpu.VMEM((HEADS * rows, HD), jnp.bfloat16),
                pltpu.VMEM(kv_weights.shape, jnp.bfloat16),
                pltpu.VMEM((n * (KVH * rows + HALF), HD), jnp.bfloat16),
                pltpu.VMEM((n, 8, rows), jnp.int32),
                pltpu.VMEM((HEADS, rows), jnp.float32),
                pltpu.VMEM((HEADS, rows), jnp.float32),
                pltpu.VMEM((HEADS, HD, rows), jnp.float32),
                pltpu.SemaphoreType.DMA,
                pltpu.SemaphoreType.DMA((HEADS,)),
                pltpu.SemaphoreType.DMA((depth // chunk,)),
                pltpu.SemaphoreType.DMA((n,)),
                pltpu.SemaphoreType.DMA((n,)),
                pltpu.SemaphoreType.DMA((n,)),
                pltpu.SemaphoreType.DMA((n,)),
                pltpu.SemaphoreType.DMA((n,)),
            ],
            compiler_params=pltpu.CompilerParams(collective_id=0, has_side_effects=True),
        )(labels.reshape(1, rows), doc_lengths, key_gains, hidden_rows, queries, kv_weights)

    in_specs = (
        P(("groups", "tok"), None),
        P(("groups", "tok"), None),
        P(("groups", "tok")),
        P("groups"),
        P(),
        P(),
    )
    out_specs = P(("groups", "tok"), None)
    return jax.shard_map(shards, mesh=mesh, in_specs=in_specs, out_specs=out_specs, check_vma=False)
```

```python
import functools
import math

import jax
import jax.numpy as jnp
from jax import lax
from jax.experimental import pallas as pl
from jax.experimental.pallas import tpu as pltpu
from jax.sharding import PartitionSpec as P

HEADS = 14
KVH = 2
HD = 128
GROUPS_PER = HEADS // KVH
HALF = KVH * HD
MESH = pl.DeviceIdType.MESH
NEG = -1e30


def kernel(
    n,
    chunk,
    labels_ref,
    lengths_ref,
    gains_ref,
    hidden_hbm,
    queries_hbm,
    weights_hbm,
    out_ref,
    hidden,
    query,
    weights,
    held,
    zeros_at,
    peak,
    summed,
    accum,
    in_sem,
    query_sem,
    weight_sem,
    send_sem,
    recv_sem,
    pass_sem,
    zsend_sem,
    zrecv_sem,
):
    rows, depth = hidden.shape
    total_len = n * rows
    me = lax.axis_index("tok")
    core = lax.rem(me, 2)
    partner = me + 1 - 2 * core
    split = n // 2 - 1
    upper = me >= split
    low = jnp.where(upper, split, 0)
    high = jnp.where(upper, n, split)
    paired = (partner >= low) & (partner < high)
    lone = jnp.where(upper, split, split - 1)
    unused = jnp.where(upper, split - 1, split)

    size = HALF // HD * rows + HALF

    def block(j):
        return pl.ds(pl.multiple_of(j * size, size), size)

    ksize = KVH * rows

    def half_of(j, half):
        return pl.ds(pl.multiple_of(j * size + half * ksize, 16), HALF if half else ksize)

    def part_of(j, at, length):
        return pl.ds(pl.multiple_of(j * size + at, 16), length)

    hidden_copy = pltpu.make_async_copy(hidden_hbm, hidden, in_sem)
    hidden_copy.start()
    chunks = depth // chunk
    weight_copies = []
    for half in range(2):
        for i in range(chunks):
            part = (slice(None), pl.ds(i * chunk, chunk), pl.ds(half * HALF, HALF))
            copy = pltpu.make_async_copy(
                weights_hbm.at[part], weights.at[part], weight_sem.at[half * chunks + i]
            )
            copy.start()
            weight_copies.append(copy)
    query_copies = []
    for h in range(HEADS):
        copy = pltpu.make_async_copy(
            queries_hbm.at[:, pl.ds(h * HD, HD)],
            query.at[pl.ds(h * rows, rows), :],
            query_sem.at[h],
        )
        copy.start()
        query_copies.append(copy)

    offset = me * rows
    lane_pos = offset + lax.broadcasted_iota(jnp.int32, (1, rows), 1)
    labels = labels_ref[...]
    first_lane = jnp.zeros((1, rows), jnp.int32)
    last_lane = jnp.full((1, rows), total_len, jnp.int32)
    end = jnp.int32(0)
    for i in range(lengths_ref.shape[0]):
        end = end + lengths_ref[i]
        first_lane = jnp.maximum(first_lane, jnp.where(end <= lane_pos, end, 0))
        last_lane = jnp.minimum(last_lane, jnp.where(end > lane_pos, end, total_len))
    last_lane = last_lane - 1
    row_at = lax.broadcasted_iota(jnp.int32, (rows, rows), 0)
    lane_at = lax.broadcasted_iota(jnp.int32, (rows, rows), 1)
    diagonal = row_at == lane_at

    zero_lane = jnp.where(labels == 0, lane_pos, total_len)
    def to_rows(lane_values):
        spread = jnp.where(diagonal, jnp.broadcast_to(lane_values, (rows, rows)), 0)
        return jnp.sum(spread, axis=1, keepdims=True)

    label = to_rows(labels)
    local_zero = jnp.min(
        jnp.where(row_at >= lane_at, to_rows(zero_lane), total_len), axis=0, keepdims=True
    )
    earliest = jnp.min(zero_lane, axis=1, keepdims=True)
    zeros_at[...] = jnp.full(zeros_at.shape, total_len, jnp.int32)
    zeros_at[me] = jnp.broadcast_to(earliest, (8, rows))
    held[block(unused), :] = jnp.zeros((size, HD), jnp.bfloat16)
    peak[...] = jnp.full(peak.shape, NEG, jnp.float32)
    summed[...] = jnp.zeros(summed.shape, jnp.float32)
    accum[...] = jnp.zeros(accum.shape, jnp.float32)

    barrier = pltpu.get_barrier_semaphore()

    @pl.loop(low, high)
    def _(d):
        @pl.when(d != me)
        def _():
            pl.semaphore_signal(barrier, inc=1, device_id={"tok": d}, device_id_type=MESH)

    def zero_copy(source, target):
        return pltpu.make_async_remote_copy(
            src_ref=zeros_at.at[source],
            dst_ref=zeros_at.at[source],
            send_sem=zsend_sem.at[target],
            recv_sem=zrecv_sem.at[source],
            device_id={"tok": target},
            device_id_type=MESH,
        )

    def kv_copy(source, target, half, sem):
        return pltpu.make_async_remote_copy(
            src_ref=held.at[half_of(source, half), :],
            dst_ref=held.at[half_of(source, half), :],
            send_sem=sem,
            recv_sem=recv_sem.at[half * n + source],
            device_id={"tok": target},
            device_id_type=MESH,
        )

    def own_copy(source, target, half):
        return kv_copy(source, target, half, send_sem.at[half * n + target])

    def pass_copy(source, half):
        return kv_copy(source, partner, half, pass_sem.at[half * n + source])

    def own_target(d):
        same = lax.rem(d, 2) == core
        return (d != me) & (same | (d == partner) | (d == lone))

    count = high - low

    def send(half):
        @pl.loop(1, count)
        def _(k):
            d = low + lax.rem(me - low - k + count, count)

            @pl.when(own_target(d))
            def _():
                own_copy(me, d, half).start()

    hidden_copy.wait()
    chosen = label == 1
    for half in range(2):
        columns = pl.ds(half * HALF, HALF)
        projected = [jnp.zeros((rows, HALF), jnp.float32) for _ in range(2)]
        for i in range(chunks):
            weight_copies[half * chunks + i].wait()
            part = pl.ds(i * chunk, chunk)
            for tower in range(2):
                projected[tower] = projected[tower] + jnp.dot(
                    hidden[:, part],
                    weights[tower, part, columns],
                    preferred_element_type=jnp.float32,
                )
            if half == 0 and i == chunks // 2:
                pl.semaphore_wait(barrier, high - low - 1)

                @pl.loop(low, me)
                def _(d):
                    zero_copy(me, d).start()

        mine = jnp.where(chosen, projected[1], projected[0])
        for g in range(KVH):
            part = mine[:, g * HD : (g + 1) * HD]
            if half == 0:
                gains = jnp.where(chosen, gains_ref[1:2, :], gains_ref[0:1, :])
                square_mean = jnp.mean(part * part, axis=-1, keepdims=True)
                part = part * lax.rsqrt(square_mean + 1e-06) * gains
                held[part_of(me, g * rows, rows), :] = part.astype(jnp.bfloat16)
            else:
                held[part_of(me, ksize + g * HD, HD), :] = part.T.astype(jnp.bfloat16)
        send(half)

    @pl.loop(me + 1, high)
    def _(d):
        zero_copy(d, me).wait_recv()

    device_at = lax.broadcasted_iota(jnp.int32, zeros_at.shape, 0)
    later = jnp.min(jnp.where(device_at > me, zeros_at[...], total_len), axis=0)
    later = later[0:1, 0:1]
    zero_next = jnp.minimum(local_zero, later)
    reach = jnp.where(labels == 1, jnp.minimum(last_lane, zero_next - 1), lane_pos)
    for copy in query_copies:
        copy.wait()

    factor_of = (1.0 / HD**0.5) * math.log2(math.e)
    chip_low = low // 2
    chip_count = (high + 1) // 2 - chip_low
    my_chip = me // 2
    pair = 2 * rows

    def chip_at(t):
        return chip_low + lax.rem(my_chip - chip_low + t, chip_count)

    def relay(t):
        same = 2 * chip_at(t) + core

        @pl.when((t < chip_count) & (same != me) & (same >= low) & (same < high))
        def _():
            for half in range(2):
                own_copy(same, me, half).wait_recv()

                @pl.when(paired)
                def _():
                    pass_copy(same, half).start()

    @pl.loop(0, chip_count)
    def _(t):
        chip = chip_at(t)
        other = 2 * chip + 1 - core

        @pl.when((other >= low) & (other < high))
        def _():
            for half in range(2):
                own_copy(other, me, half).wait_recv()

        relay(t + 1)

        key_pos = chip * pair + lax.broadcasted_iota(jnp.int32, (pair, rows), 0)
        visible = (key_pos >= first_lane) & (key_pos <= reach)
        bias = jnp.where(visible, 0.0, NEG)
        for g in range(KVH):
            keys = jnp.concatenate(
                [held[part_of(2 * chip + i, g * rows, rows), :] for i in range(2)], axis=0
            )
            values = jnp.concatenate(
                [held[part_of(2 * chip + i, KVH * rows + g * HD, HD), :] for i in range(2)], axis=1
            )
            for h in range(g * GROUPS_PER, (g + 1) * GROUPS_PER):
                scores = lax.dot_general(
                    keys,
                    query[h * rows : (h + 1) * rows, :],
                    (((1,), (1,)), ((), ())),
                    preferred_element_type=jnp.float32,
                )
                scores = scores + bias
                old_peak = peak[h : h + 1, :]
                new_peak = jnp.maximum(old_peak, jnp.max(scores, axis=0, keepdims=True))
                weight = jnp.exp2((scores - new_peak) * factor_of)
                factor = jnp.exp2((old_peak - new_peak) * factor_of)
                peak[h : h + 1, :] = new_peak
                summed[h : h + 1, :] = summed[h : h + 1, :] * factor + jnp.sum(
                    weight, axis=0, keepdims=True
                )
                mixed = jnp.dot(
                    values, weight.astype(jnp.bfloat16), preferred_element_type=jnp.float32
                )
                accum[h] = accum[h] * factor + mixed

    for h in range(HEADS):
        result = accum[h] * (1.0 / summed[h : h + 1, :])
        out_ref[:, h * HD : (h + 1) * HD] = result.T.astype(out_ref.dtype)

    @pl.loop(low, me)
    def _(d):
        zero_copy(me, d).wait_send()

    @pl.loop(low, high)
    def _(d):
        for half in range(2):

            @pl.when(own_target(d))
            def _():
                own_copy(me, d, half).wait_send()

            @pl.when(paired & (d != me) & (lax.rem(d, 2) == core))
            def _():
                pass_copy(d, half).wait_send()


def solution(mesh):
    n = mesh.shape["tok"]

    def shards(hidden_rows, queries, labels, doc_lengths, kv_weights, key_gains):
        rows, depth = hidden_rows.shape
        assert rows == HD
        chunk = math.gcd(depth, 512)
        any_space = pl.BlockSpec(memory_space=pl.ANY)
        vmem = pl.BlockSpec(memory_space=pltpu.VMEM)
        return pl.pallas_call(
            functools.partial(kernel, n, chunk),
            out_shape=jax.ShapeDtypeStruct(queries.shape, jnp.bfloat16),
            in_specs=[
                vmem,
                pl.BlockSpec(memory_space=pltpu.SMEM),
                vmem,
                any_space,
                any_space,
                any_space,
            ],
            out_specs=vmem,
            scratch_shapes=[
                pltpu.VMEM((rows, depth), jnp.bfloat16),
                pltpu.VMEM((HEADS * rows, HD), jnp.bfloat16),
                pltpu.VMEM(kv_weights.shape, jnp.bfloat16),
                pltpu.VMEM((n * (KVH * rows + HALF), HD), jnp.bfloat16),
                pltpu.VMEM((n, 8, rows), jnp.int32),
                pltpu.VMEM((HEADS, rows), jnp.float32),
                pltpu.VMEM((HEADS, rows), jnp.float32),
                pltpu.VMEM((HEADS, HD, rows), jnp.float32),
                pltpu.SemaphoreType.DMA,
                pltpu.SemaphoreType.DMA((HEADS,)),
                pltpu.SemaphoreType.DMA((2 * depth // chunk,)),
                pltpu.SemaphoreType.DMA((2 * n,)),
                pltpu.SemaphoreType.DMA((2 * n,)),
                pltpu.SemaphoreType.DMA((2 * n,)),
                pltpu.SemaphoreType.DMA((n,)),
                pltpu.SemaphoreType.DMA((n,)),
            ],
            compiler_params=pltpu.CompilerParams(collective_id=0, has_side_effects=True),
        )(labels.reshape(1, rows), doc_lengths, key_gains, hidden_rows, queries, kv_weights)

    in_specs = (
        P(("groups", "tok"), None),
        P(("groups", "tok"), None),
        P(("groups", "tok")),
        P("groups"),
        P(),
        P(),
    )
    out_specs = P(("groups", "tok"), None)
    return jax.shard_map(shards, mesh=mesh, in_specs=in_specs, out_specs=out_specs, check_vma=False)
```
